128 devices in a mesh: row: 8 (over z, core), col: 16 (over x, y).
Axes of the slice: x: 4, y: 4, z: 4, core: 2. Of those that a mesh axis runs over, the one named last changes fastest.
Arguments:
- left_edge: bfloat16 [16, 3072, 3072], P('row', 'col'), may hold values from -6 to 6
- right_edge: bfloat16 [16, 3072, 3072], P('row', 'col'), may hold values from -0.109375 to 0.109375
- projector: bfloat16 [16, 3072, 64], P('row'), may hold values from -0.109375 to 0.109375
- sector_size: int32 [16], P('row'), may hold values from 1 to 3072, 30720 in all
Outputs:
- enlarged: float32 [16, 3072, 3072], P('row', 'col')
- new_corner: float32 [16, 64, 64], P('row')
The draws below stay inside these ranges and needn't reach their ends.
All inputs are finite; a program needn't handle non-finite values. No bound on the sum of `sector_size` on one device may be relied on, other than what follows from the above.
Results may differ from the reference program's by a relative error of at most 0.0003.
Values may be sent and summed in bfloat16 or wider, within the bound.
No kernel may reach another device: no remote copies, remote signals or barrier semaphores. Data moves between devices by JAX's collectives and lax.ppermute only.
A program may use at most 128 MiB of HBM per device.

```python
import math
import jax
import jax.numpy as jnp
import numpy as np
from jax import lax

B = 3072
K = 3072
KEEP = 64
S = 16
TOTAL_LIVE = 30720


def block_levels(key, extent, cuts, smallest, high):
    factor_of, own = 1.0, jax.random.fold_in(key, 6)
    for axis_at, shards_of in cuts:
        steps = jnp.exp(jax.random.uniform(jax.random.fold_in(own, axis_at), (shards_of,), jnp.float32, smallest / len(cuts), high / len(cuts)))
        factor_of = factor_of * jnp.repeat(steps, extent[axis_at] // shards_of).reshape([-1 if axis == axis_at else 1 for axis in range(len(extent))])
    return factor_of


def length_profile(number_of, total, bound, slope):
    loads = [(1 << 20) // math.isqrt(standing ** slope) + 1 for standing in range(2, number_of + 1)]
    rest, given = total - bound - (number_of - 1), [1] * (number_of - 1)
    while rest > 0:
        free = [i for i in range(number_of - 1) if given[i] < bound]
        whole, budget = sum([loads[i] for i in free]), rest
        for i in free:
            extra = min(bound - given[i], max(1, budget * loads[i] // whole), rest)
            given[i] = given[i] + extra
            rest = rest - extra
    return np.array([bound] + given)


def uneven_parts(own_key, amount, total, bound, slope):
    if amount == 2:
        one = jax.random.randint(own_key, (), max(1, total - bound), min(bound, total - 1) + 1)
        return jnp.stack([one, total - one])
    sizes = jnp.asarray(length_profile(amount, total, bound, slope), jnp.int32)
    twos = (amount - 1) // 2
    source_of, sink = sizes[1:1 + 2 * twos:2], sizes[2:2 + 2 * twos:2]
    room = jnp.minimum(source_of - 1, bound - sink)
    shifted = jax.random.randint(jax.random.fold_in(own_key, 1), (twos,), 0, 1 << 20) % (room + 1)
    sizes = sizes.at[1:1 + 2 * twos:2].set(source_of - shifted).at[2:2 + 2 * twos:2].set(sink + shifted)
    return sizes[jax.random.permutation(jax.random.fold_in(own_key, 2), amount)]


def normal_values(own_key, extent, spread, bound, split=(), kind=jnp.bfloat16):
    loudness = block_levels(own_key, extent, split, -0.22, 0.18) if split else 1.0
    entries = jax.random.normal(own_key, extent, jnp.float32) * spread * loudness
    return jnp.minimum(jnp.maximum(entries, -bound), bound).astype(kind)


def setup_inputs(seed: int = 0) -> dict:
    arg_keys = jax.random.split(jax.random.key(seed), 5)
    return {
        "left_edge": normal_values(arg_keys[0], (S, B, K), 1.0, 6.0, ((0, 8), (1, 16))),
        "right_edge": normal_values(arg_keys[1], (S, K, B), K ** -0.5, 0.109375, ((0, 8), (1, 16))),
        "projector": normal_values(arg_keys[2], (S, B, KEEP), B ** -0.5, 0.109375, ((0, 8),)),
        "sector_size": uneven_parts(arg_keys[3], S, TOTAL_LIVE, B, 2).astype(jnp.int32),
    }


def reference(left_edge, right_edge, projector, sector_size):
    count = left_edge.shape[0]
    width = left_edge.shape[1]
    kept = projector.shape[2]
    states = jnp.arange(width, dtype=jnp.int32)

    def one_sector(sector):
        enlarged = jnp.dot(left_edge[sector], right_edge[sector], preferred_element_type=jnp.float32)
        live = (states < sector_size[sector]).astype(jnp.float32)
        masked = projector[sector].astype(jnp.float32) * live[:, None]
        inner = jnp.dot(enlarged, masked, precision=lax.Precision.HIGHEST)
        return (enlarged, jnp.dot(masked.T, inner, precision=lax.Precision.HIGHEST))
    enlarged, corner = lax.map(one_sector, jnp.arange(count, dtype=jnp.int32))
    total = jnp.sum(corner * corner)
    return (enlarged, corner * lax.rsqrt(total / (count * kept * kept) + 1e-06))
```

```python
import jax
import jax.numpy as jnp
from jax import lax
from jax.experimental import pallas as pl
from jax.experimental.pallas import tpu as pltpu
from jax.sharding import PartitionSpec as P

SIDE = 4
CHUNKS = 3


def product(offsets, left, own, below, above, low, high, widths):
    rows, depth = left.shape[1:]
    full = own.shape[2]
    pieces = [(i, p) for i, ref in enumerate((own, below, above, low, high)) for p in range(ref.shape[0])]

    def kernel(off, l, r0, r1, r2, r3, r4, *rest):
        outs, (scratch, sems) = rest[:-2], rest[-2:]
        refs = (r0, r1, r2, r3, r4)
        copies = []
        for n, (i, p) in enumerate(pieces):
            at = pl.multiple_of(off[n], 64)
            copies.append(pltpu.make_async_copy(refs[i].at[p], scratch.at[pl.ds(at, rows)], sems.at[n]))
        for copy in copies:
            copy.start()
        for copy in copies:
            copy.wait()
        lhs = l[...].reshape(SIDE * rows, depth)
        start = 0
        for out, width in zip(outs, widths):
            got = jnp.dot(lhs, scratch[:, start:start + width], preferred_element_type=jnp.float32)
            out[...] = got.reshape(SIDE, rows, width)
            start += width

    anywhere = pl.BlockSpec(memory_space=pl.ANY)
    inside = pl.BlockSpec(memory_space=pltpu.VMEM)
    return pl.pallas_call(
        kernel,
        in_specs=[pl.BlockSpec(memory_space=pltpu.SMEM), inside] + [anywhere] * 5,
        out_specs=[inside] * len(widths),
        out_shape=[jax.ShapeDtypeStruct((SIDE, rows, width), jnp.float32) for width in widths],
        scratch_shapes=[pltpu.VMEM((depth, full), jnp.bfloat16), pltpu.SemaphoreType.DMA((len(pieces),))],
        compiler_params=pltpu.CompilerParams(vmem_limit_bytes=40 << 20),
    )(offsets, left, own, below, above, low, high)


def solution(mesh):
    n_row, n_col = mesh.shape["row"], mesh.shape["col"]

    def pairs(move):
        found = []
        for row in range(n_row):
            for col in range(n_col):
                cx, cy = col // SIDE, col % SIDE
                g, h = (cy, cx) if row % 2 else (cx, cy)
                to, g, h = move(row, g, h)
                cx, cy = (h, g) if row % 2 else (g, h)
                if to != row:
                    cx, cy = col // SIDE, col % SIDE
                found.append((row * n_col + col, to * n_col + cx * SIDE + cy))
        return found

    along_g = {p: pairs(lambda row, g, h, p=p: (row, g ^ p, h)) for p in (1, 2, 3)}
    along_h = {p: pairs(lambda row, g, h, p=p: (row, g, h ^ p)) for p in (1, 2)}
    up = pairs(lambda row, g, h: (row, g, (h + 1) % SIDE))
    down = pairs(lambda row, g, h: (row, g, (h - 1) % SIDE))
    across = {p: pairs(lambda row, g, h, p=p: (row ^ p, g, h)) for p in (1, 2, 4)}

    def send(value, table):
        return lax.ppermute(value, ("row", "col"), table)

    def body(left_edge, right_edge, projector, sector_size):
        count, rows, depth = left_edge.shape
        kept = projector.shape[2]
        half = depth // 2
        width = half // CHUNKS
        odd = lax.axis_index("row") % 2
        col = lax.axis_index("col")
        cx, cy = col // SIDE, col % SIDE
        g = jnp.where(odd == 1, cy, cx)
        h = jnp.where(odd == 1, cx, cy)
        owner = lambda gg, hh: jnp.where(odd == 1, hh * SIDE + gg, gg * SIDE + hh)

        states = jnp.arange(depth, dtype=jnp.int32)
        live = (states[None, :] < sector_size[:, None]).astype(jnp.bfloat16)
        masked = projector * live[:, :, None]

        seen = jnp.einsum("skj,sjq->skq", right_edge, masked, preferred_element_type=jnp.float32)
        top = lax.reduce_precision(seen, exponent_bits=8, mantissa_bits=7)
        shadow = jnp.concatenate([top, seen - top], axis=2).astype(jnp.bfloat16)

        sector = g // 2
        mine = lax.dynamic_index_in_dim(left_edge, sector, 0, keepdims=False)
        other = lax.dynamic_index_in_dim(left_edge, 1 - sector, 0, keepdims=False)

        def part(p, c):
            to = g ^ p
            start = (to % 2) * half + c * width
            got = lax.dynamic_slice(right_edge, (to // 2, 0, start), (1, rows, width))[0]
            if c == 0:
                got = jnp.concatenate([got, lax.dynamic_index_in_dim(shadow, to // 2, 0, keepdims=False)], axis=1)
            return got

        near = send(other, along_g[3])
        paired = send(mine, along_g[1])
        far = send(near, along_g[1])
        left = jnp.stack([mine, paired, far, near])

        hs = [h, (h - 1) % SIDE, (h + 1) % SIDE, (h + 2) % SIDE]
        offsets = jnp.stack([owner(g ^ p, hh) * rows for hh in hs for p in range(SIDE)]).astype(jnp.int32)

        enlarged = jnp.zeros((count, rows, depth), jnp.float32)
        inner = None
        for c in range(CHUNKS):
            own = jnp.stack([part(0, c)] + [send(part(p, c), along_g[p]) for p in (1, 2, 3)])
            below = send(own, up)
            above = send(own, down)
            low = send(below[:2], up)
            high = send(above[2:], down)
            widths = (width,) if c else (width, 2 * kept)
            out = product(offsets, left, own, below, above, low, high, widths)
            if c == 0:
                inner = out[1]
            for p in range(SIDE):
                block = out[0][p]
                if p:
                    block = send(block, along_g[p])
                start = ((g ^ p) % 2) * half + c * width
                enlarged = lax.dynamic_update_slice(enlarged, block[None], ((g ^ p) // 2, 0, start))

        inner = inner[:, :, :kept] + inner[:, :, kept:]
        ours = lax.dynamic_index_in_dim(masked, sector, 0, keepdims=False)
        terms = []
        for p in range(SIDE):
            chosen = lax.dynamic_slice_in_dim(ours, owner(g ^ p, h) * rows, rows, 0).astype(jnp.float32)
            terms.append(jnp.einsum("ip,iq->pq", chosen, inner[p], precision=lax.Precision.HIGHEST))
        corner = (terms[0] + terms[1]) + (terms[2] + terms[3])
        for p in (1, 2):
            corner = corner + send(corner, along_h[p])
        beside = send(corner, along_g[2])
        corner = jnp.where(sector == 0, jnp.stack([corner, beside]), jnp.stack([beside, corner]))
        total = jnp.broadcast_to(jnp.sum(corner * corner), (8, 128))
        for p in (1, 2, 4):
            total = total + send(total, across[p])
        entries = n_row * count * kept * kept
        return enlarged, corner * lax.rsqrt(total[0, 0] / entries + 1e-06)

    placed = (P("row", "col", None), P("row", "col", None), P("row", None, None), P("row"))
    return jax.shard_map(
        body,
        mesh=mesh,
        in_specs=placed,
        out_specs=(P("row", "col", None), P("row", None, None)),
        check_vma=False,
    )
```

```python
import jax
import jax.numpy as jnp
from jax import lax
from jax.experimental import pallas as pl
from jax.experimental.pallas import tpu as pltpu
from jax.sharding import PartitionSpec as P

SIDE = 4
CHUNKS = 2


def product(offsets, left, pieces, widths):
    rows, depth = left.shape[1:]
    full = pieces[0].shape[2]
    where = [(i, p) for i, piece in enumerate(pieces) for p in range(piece.shape[0])]

    def kernel(off, l, *rest):
        refs, outs = rest[:len(pieces)], rest[len(pieces):-2]
        scratch, sems = rest[-2:]
        copies = []
        for n, (i, p) in enumerate(where):
            at = pl.multiple_of(off[n], 64)
            copies.append(pltpu.make_async_copy(refs[i].at[p], scratch.at[pl.ds(at, rows)], sems.at[n]))
        for copy in copies:
            copy.start()
        for copy in copies:
            copy.wait()
        lhs = l[...].reshape(SIDE * rows, depth)
        start = 0
        for k, width in enumerate(widths):
            got = jnp.dot(lhs, scratch[:, start:start + width], preferred_element_type=jnp.float32)
            for p in range(SIDE):
                outs[k * SIDE + p][...] = got[p * rows:(p + 1) * rows]
            start += width

    anywhere = pl.BlockSpec(memory_space=pl.ANY)
    inside = pl.BlockSpec(memory_space=pltpu.VMEM)
    return pl.pallas_call(
        kernel,
        in_specs=[pl.BlockSpec(memory_space=pltpu.SMEM), inside] + [anywhere] * len(pieces),
        out_specs=[inside] * (SIDE * len(widths)),
        out_shape=[jax.ShapeDtypeStruct((rows, width), jnp.float32) for width in widths for _ in range(SIDE)],
        scratch_shapes=[pltpu.VMEM((depth, full), jnp.bfloat16), pltpu.SemaphoreType.DMA((len(where),))],
        compiler_params=pltpu.CompilerParams(vmem_limit_bytes=32 << 20),
    )(offsets, left, *pieces)


def place(spots, blocks, shape, into=None):
    rows, width = blocks[0].shape
    n = len(blocks)

    def kernel(at, *rest):
        out, sems = rest[-2:]
        copies = []
        for k in range(n):
            start = pl.multiple_of(at[n + k], 128)
            copies.append(pltpu.make_async_copy(rest[k], out.at[at[k], :, pl.ds(start, width)], sems.at[k]))
        for copy in copies:
            copy.start()
        for copy in copies:
            copy.wait()

    anywhere = pl.BlockSpec(memory_space=pl.ANY)
    inside = pl.BlockSpec(memory_space=pltpu.VMEM)
    given = list(blocks) + ([] if into is None else [into])
    return pl.pallas_call(
        kernel,
        in_specs=[pl.BlockSpec(memory_space=pltpu.SMEM)] + [inside] * n + [anywhere] * (len(given) - n),
        out_specs=anywhere,
        out_shape=jax.ShapeDtypeStruct(shape, jnp.float32),
        scratch_shapes=[pltpu.SemaphoreType.DMA((n,))],
        input_output_aliases={} if into is None else {n + 1: 0},
        compiler_params=pltpu.CompilerParams(vmem_limit_bytes=8 << 20),
    )(spots, *given)


def solution(mesh):
    n_row, n_col = mesh.shape["row"], mesh.shape["col"]

    def pairs(move):
        found = []
        for row in range(n_row):
            for col in range(n_col):
                cx, cy = col // SIDE, col % SIDE
                g, h = (cy, cx) if row % 2 else (cx, cy)
                to, g, h = move(row, g, h)
                cx, cy = (h, g) if row % 2 else (g, h)
                if to != row:
                    cx, cy = col // SIDE, col % SIDE
                found.append((row * n_col + col, to * n_col + cx * SIDE + cy))
        return found

    along_g = {p: pairs(lambda row, g, h, p=p: (row, g ^ p, h)) for p in (1, 2, 3)}
    along_h = {p: pairs(lambda row, g, h, p=p: (row, g, h ^ p)) for p in (1, 2)}
    up = pairs(lambda row, g, h: (row, g, (h + 1) % SIDE))
    down = pairs(lambda row, g, h: (row, g, (h - 1) % SIDE))
    across = {p: pairs(lambda row, g, h, p=p: (row ^ p, g, h)) for p in (1, 2, 4)}

    def send(value, table, name):
        with jax.named_scope(name):
            return lax.ppermute(value, ("row", "col"), table)

    def after(value, *others):
        return lax.optimization_barrier((value, *others))[0]

    def body(left_edge, right_edge, projector, sector_size):
        count, rows, depth = left_edge.shape
        kept = projector.shape[2]
        half = depth // 2
        width = half // CHUNKS
        odd = lax.axis_index("row") % 2
        col = lax.axis_index("col")
        cx, cy = col // SIDE, col % SIDE
        g = jnp.where(odd == 1, cy, cx)
        h = jnp.where(odd == 1, cx, cy)
        owner = lambda gg, hh: jnp.where(odd == 1, hh * SIDE + gg, gg * SIDE + hh)

        states = jnp.arange(depth, dtype=jnp.int32)
        live = (states[None, :] < sector_size[:, None]).astype(jnp.bfloat16)
        masked = projector * live[:, :, None]

        seen = jnp.einsum("skj,sjq->skq", right_edge, masked, preferred_element_type=jnp.float32)
        top = lax.reduce_precision(seen, exponent_bits=8, mantissa_bits=7)
        shadow = jnp.concatenate([top, seen - top], axis=2).astype(jnp.bfloat16)

        sector = g // 2
        mine = lax.dynamic_index_in_dim(left_edge, sector, 0, keepdims=False)
        other = lax.dynamic_index_in_dim(left_edge, 1 - sector, 0, keepdims=False)

        def part(p):
            to = g ^ p
            got = lax.dynamic_slice(right_edge, (to // 2, 0, (to % 2) * half), (1, rows, half))[0]
            return jnp.concatenate([lax.dynamic_index_in_dim(shadow, to // 2, 0, keepdims=False), got], axis=1)

        gs = [g ^ p for p in range(SIDE)]
        hs = [h, (h - 1) % SIDE, (h + 1) % SIDE, (h + 2) % SIDE]
        offsets = jnp.stack([owner(gg, hh) * rows for hh in hs for gg in gs]).astype(jnp.int32)

        left = [mine] + [send(mine if p == 1 else other, along_g[p], f"left{p}") for p in (1, 2, 3)]
        blocks = [part(0)] + [send(part(p), along_g[p], f"right{p}") for p in (1, 2, 3)]

        extra = 2 * kept

        def cut(c):
            first = extra + c * width if c else 0
            return jnp.stack([block[:, first:extra + (c + 1) * width] for block in blocks])

        def spots(c):
            return jnp.stack([gg // 2 for gg in gs] + [(gg % 2) * half + c * width for gg in gs]).astype(jnp.int32)

        own0 = after(cut(0), left[1], left[3])
        below0, above0 = send(own0, up, "up0"), send(own0, down, "down0")
        beyond0 = send(after(below0, left[2]), up, "forward0")
        own1 = after(cut(1), below0, above0)
        below1, above1 = send(own1, up, "up1"), send(own1, down, "down1")
        left = jnp.stack(left)
        out = product(offsets, left, (own0, below0, above0, beyond0), (extra, width))
        inner, out0 = out[:SIDE], out[SIDE:]
        beyond1 = send(above1, down, "forward1")
        out0 = [out0[0]] + [send(out0[p], along_g[p], f"back0{p}") for p in (1, 2, 3)]
        beyond1 = after(beyond1, *out0[1:])
        out1 = product(offsets, left, (own1, below1, above1, beyond1), (width,))
        enlarged = place(spots(0), out0, (count, rows, depth))
        out1 = [out1[0]] + [send(out1[p], along_g[p], f"back1{p}") for p in (1, 2, 3)]
        enlarged = place(spots(1), out1, (count, rows, depth), enlarged)

        inner = [got[:, :kept] + got[:, kept:] for got in inner]
        ours = lax.dynamic_index_in_dim(masked, sector, 0, keepdims=False)
        terms = []
        for p in range(SIDE):
            chosen = lax.dynamic_slice_in_dim(ours, owner(g ^ p, h) * rows, rows, 0).astype(jnp.float32)
            terms.append(jnp.einsum("ip,iq->pq", chosen, inner[p], precision=lax.Precision.HIGHEST))
        corner = (terms[0] + terms[1]) + (terms[2] + terms[3])
        for p in (1, 2):
            corner = corner + send(corner, along_h[p], f"corner{p}")
        beside = send(corner, along_g[2], "beside")
        corner = jnp.where(sector == 0, jnp.stack([corner, beside]), jnp.stack([beside, corner]))
        total = jnp.broadcast_to(jnp.sum(corner * corner), (8, 128))
        for p in (1, 2, 4):
            total = total + send(total, across[p], f"total{p}")
        entries = n_row * count * kept * kept
        return enlarged, corner * lax.rsqrt(total[0, 0] / entries + 1e-06)

    placed = (P("row", "col", None), P("row", "col", None), P("row", None, None), P("row"))
    return jax.shard_map(
        body,
        mesh=mesh,
        in_specs=placed,
        out_specs=(P("row", "col", None), P("row", None, None)),
        check_vma=False,
    )
```

```python
import jax
import jax.numpy as jnp
from jax import lax
from jax.experimental import pallas as pl
from jax.experimental.pallas import tpu as pltpu
from jax.sharding import PartitionSpec as P

SIDE = 4


def start_gather(refs, where, off, scratch, sems, rows, at, sides):
    copies = []
    for k, (first, last) in enumerate(sides):
        column = []
        for n, (i, p) in enumerate(where):
            into = scratch.at[pl.ds(pl.multiple_of(off[n], 64), rows), first:last]
            source = refs[i].at[p, :, at[i] + first:at[i] + last]
            column.append(pltpu.make_async_copy(source, into, sems.at[k, n]))
        copies.append(column)
    for column in copies:
        for copy in column:
            copy.start()
    return copies


def product(offsets, lefts, pieces, at, width):
    rows, depth = lefts[0].shape
    middle = width // 256 * 128
    sides = ((0, middle), (middle, width))
    where = [(i, p) for i, piece in enumerate(pieces) for p in range(piece.shape[0])]
    n_left = len(lefts)

    def kernel(off, *rest):
        ls, refs, outs = rest[:n_left], rest[n_left:n_left + len(pieces)], rest[n_left + len(pieces):-4]
        lhs, scratch, left_sems, sems = rest[-4:]
        loads = [pltpu.make_async_copy(ls[p], lhs.at[pl.ds(p * rows, rows)], left_sems.at[p]) for p in range(n_left)]
        for copy in loads:
            copy.start()
        copies = start_gather(refs, where, off, scratch, sems, rows, at, sides)
        for copy in loads:
            copy.wait()
        for column, (first, last) in zip(copies, sides):
            for copy in column:
                copy.wait()
            got = jnp.dot(lhs[...], scratch[:, first:last], preferred_element_type=jnp.float32)
            for p in range(n_left):
                outs[p][:, first:last] = got[p * rows:(p + 1) * rows]

    outside = pl.BlockSpec(memory_space=pltpu.HBM)
    inside = pl.BlockSpec(memory_space=pltpu.VMEM)
    return pl.pallas_call(
        kernel,
        in_specs=[pl.BlockSpec(memory_space=pltpu.SMEM)] + [outside] * (n_left + len(pieces)),
        out_specs=[inside] * n_left,
        out_shape=[jax.ShapeDtypeStruct((rows, width), jnp.float32)] * n_left,
        scratch_shapes=[
            pltpu.VMEM((n_left * rows, depth), jnp.bfloat16),
            pltpu.VMEM((depth, width), jnp.bfloat16),
            pltpu.SemaphoreType.DMA((n_left,)),
            pltpu.SemaphoreType.DMA((2, len(where))),
        ],
        cost_estimate=pl.CostEstimate(
            flops=2 * n_left * rows * depth * width,
            bytes_accessed=2 * depth * (n_left * rows + width) + 4 * n_left * rows * width,
            transcendentals=0,
        ),
        compiler_params=pltpu.CompilerParams(vmem_limit_bytes=56 << 20),
    )(offsets, *lefts, *pieces)


def share(offsets, lefts, chosen, pieces, extra):
    rows, depth = lefts[0].shape
    kept = extra // 2
    n_left = len(lefts)
    where = [(i, p) for i, piece in enumerate(pieces) for p in range(piece.shape[0])]

    def kernel(off, pick, *rest):
        ls, refs = rest[:n_left], rest[n_left:n_left + len(pieces)]
        out, lhs, scratch, left_sems, sems = rest[-5:]
        loads = [pltpu.make_async_copy(ls[p], lhs.at[pl.ds(p * rows, rows)], left_sems.at[p]) for p in range(n_left)]
        for copy in loads:
            copy.start()
        copies = start_gather(refs, where, off, scratch, sems, rows, [0] * len(pieces), ((0, extra),))
        for copy in loads + copies[0]:
            copy.wait()
        got = jnp.dot(lhs[...], scratch[...], preferred_element_type=jnp.float32)
        inner = got[:, :kept] + got[:, kept:]
        terms = []
        for p in range(n_left):
            left_over, term = inner[p * rows:(p + 1) * rows], None
            for _ in range(3):
                digit = left_over.astype(jnp.bfloat16)
                left_over = left_over - digit.astype(jnp.float32)
                part = jnp.dot(pick[p], digit, preferred_element_type=jnp.float32)
                term = part if term is None else term + part
            terms.append(term)
        out[...] = (terms[0] + terms[1]) + (terms[2] + terms[3])

    outside = pl.BlockSpec(memory_space=pltpu.HBM)
    inside = pl.BlockSpec(memory_space=pltpu.VMEM)
    return pl.pallas_call(
        kernel,
        in_specs=[pl.BlockSpec(memory_space=pltpu.SMEM), inside] + [outside] * (n_left + len(pieces)),
        out_specs=inside,
        out_shape=jax.ShapeDtypeStruct((kept, kept), jnp.float32),
        scratch_shapes=[
            pltpu.VMEM((n_left * rows, depth), jnp.bfloat16),
            pltpu.VMEM((depth, extra), jnp.bfloat16),
            pltpu.SemaphoreType.DMA((n_left,)),
            pltpu.SemaphoreType.DMA((1, len(where))),
        ],
        cost_estimate=pl.CostEstimate(
            flops=2 * n_left * rows * depth * extra,
            bytes_accessed=2 * depth * (n_left * rows + extra),
            transcendentals=0,
        ),
        compiler_params=pltpu.CompilerParams(vmem_limit_bytes=56 << 20),
    )(offsets, chosen, *lefts, *pieces)


def place(spots, blocks, shape, into=None):
    rows, width = blocks[0].shape
    n = len(blocks)

    def kernel(at, *rest):
        out, sems = rest[-2:]
        copies = []
        for k in range(n):
            start = pl.multiple_of(at[n + k], 128)
            copies.append(pltpu.make_async_copy(rest[k], out.at[at[k], :, pl.ds(start, width)], sems.at[k]))
        for copy in copies:
            copy.start()
        for copy in copies:
            copy.wait()

    anywhere = pl.BlockSpec(memory_space=pl.ANY)
    inside = pl.BlockSpec(memory_space=pltpu.VMEM)
    given = list(blocks) + ([] if into is None else [into])
    return pl.pallas_call(
        kernel,
        in_specs=[pl.BlockSpec(memory_space=pltpu.SMEM)] + [inside] * n + [anywhere] * (len(given) - n),
        out_specs=anywhere,
        out_shape=jax.ShapeDtypeStruct(shape, jnp.float32),
        scratch_shapes=[pltpu.SemaphoreType.DMA((n,))],
        input_output_aliases={} if into is None else {n + 1: 0},
        compiler_params=pltpu.CompilerParams(vmem_limit_bytes=8 << 20),
    )(spots, *given)


def solution(mesh):
    n_row, n_col = mesh.shape["row"], mesh.shape["col"]

    def pairs(move):
        found = []
        for row in range(n_row):
            for col in range(n_col):
                cx, cy = col // SIDE, col % SIDE
                g, h = (cy, cx) if row % 2 else (cx, cy)
                to, g, h = move(row, g, h)
                cx, cy = (h, g) if row % 2 else (g, h)
                if to != row:
                    cx, cy = col // SIDE, col % SIDE
                found.append((row * n_col + col, to * n_col + cx * SIDE + cy))
        return found

    along_g = {p: pairs(lambda row, g, h, p=p: (row, g ^ p, h)) for p in (1, 2, 3)}
    along_h = {p: pairs(lambda row, g, h, p=p: (row, g, h ^ p)) for p in (1, 2)}
    up = pairs(lambda row, g, h: (row, g, (h + 1) % SIDE))
    down = pairs(lambda row, g, h: (row, g, (h - 1) % SIDE))
    across_h = pairs(lambda row, g, h: (row, g, (h + 2) % SIDE))
    across = {p: pairs(lambda row, g, h, p=p: (row ^ p, g, h)) for p in (1, 2, 4)}

    def send(value, table, name):
        with jax.named_scope(name):
            return lax.ppermute(value, ("row", "col"), table)

    def after(value, *others):
        return lax.optimization_barrier((value, *others))[0]

    def body(left_edge, right_edge, projector, sector_size):
        count, rows, depth = left_edge.shape
        kept = projector.shape[2]
        half = depth // 2
        width = half // 2
        odd = lax.axis_index("row") % 2
        col = lax.axis_index("col")
        cx, cy = col // SIDE, col % SIDE
        g = jnp.where(odd == 1, cy, cx)
        h = jnp.where(odd == 1, cx, cy)
        owner = lambda gg, hh: jnp.where(odd == 1, hh * SIDE + gg, gg * SIDE + hh)

        states = jnp.arange(depth, dtype=jnp.int32)
        live = (states[None, :] < sector_size[:, None]).astype(jnp.bfloat16)
        masked = projector * live[:, :, None]

        sector = g // 2
        mine = lax.dynamic_index_in_dim(left_edge, sector, 0, keepdims=False)
        other = lax.dynamic_index_in_dim(left_edge, 1 - sector, 0, keepdims=False)

        right_edge = after(right_edge, mine, other)
        seen = jnp.einsum("skj,sjq->skq", right_edge, masked, preferred_element_type=jnp.float32)
        top = lax.reduce_precision(seen, exponent_bits=8, mantissa_bits=7)
        shadow = jnp.concatenate([top, seen - top], axis=2).astype(jnp.bfloat16)

        def part(p):
            to = g ^ p
            got = lax.dynamic_slice(right_edge, (to // 2, 0, (to % 2) * half), (1, rows, half))[0]
            return jnp.concatenate([lax.dynamic_index_in_dim(shadow, to // 2, 0, keepdims=False), got], axis=1)

        gs = [g ^ p for p in range(SIDE)]
        hs = [h, (h - 1) % SIDE, (h + 1) % SIDE, (h + 2) % SIDE]
        offsets = jnp.stack([owner(gg, hh) * rows for hh in hs for gg in gs]).astype(jnp.int32)

        left = [mine] + [send(mine if p == 1 else other, along_g[p], f"left{p}") for p in (1, 2, 3)]
        blocks = [part(0)] + [send(part(p), along_g[p], f"right{p}") for p in (1, 2, 3)]

        extra = 2 * kept

        def cut(c):
            first = extra + width if c else 0
            return jnp.stack([block[:, first:extra + (c + 1) * width] for block in blocks])

        def put(c, out, into):
            first = c * width
            spots = jnp.stack([gg // 2 for gg in gs] + [(gg % 2) * half + first for gg in gs]).astype(jnp.int32)
            return place(spots, out, (count, rows, depth), into)

        def back(c, out):
            return [out[0]] + [send(out[p], along_g[p], f"back{c}{p}") for p in (1, 2, 3)]

        ours = lax.dynamic_index_in_dim(masked, sector, 0, keepdims=False)
        chosen = jnp.stack([lax.dynamic_slice_in_dim(ours, owner(gg, h) * rows, rows, 0).T for gg in gs])

        shade = jnp.stack([block[:, :extra] for block in blocks])
        own0 = after(cut(0), left[1], left[3])
        far = send(shade, across_h, "shade")
        below0, above0 = send(own0, up, "up0"), send(own0, down, "down0")
        below0, above0, far, left[2] = lax.optimization_barrier((below0, above0, far, left[2]))
        own1 = cut(1)
        beyond0 = send(below0, up, "forward0")
        above1 = send(after(own1, above0), down, "down1")
        corner = share(offsets, left, chosen, (own0, below0, above0, far), extra)
        corner = corner + send(corner, along_h[1], "corner1")
        beyond0, above1, corner = lax.optimization_barrier((beyond0, above1, corner))
        below1 = send(after(own1, beyond0), up, "up1")
        beyond1 = send(above1, down, "forward1")
        corner = corner + send(corner, along_h[2], "corner2")
        skips = (extra,) * 4
        out0 = product(offsets, left, (own0, below0, above0, beyond0), skips, width)
        out0, corner = lax.optimization_barrier((out0, corner))
        out0 = back(0, out0)
        beside = send(corner, along_g[2], "beside")
        out1 = product(offsets, left, (own1, below1, above1, beyond1), (0,) * 4, width)
        out1, out0, beside = lax.optimization_barrier((out1, out0, beside))
        out1 = back(1, out1)
        enlarged = put(1, out1, put(0, out0, None))
        corner = jnp.where(sector == 0, jnp.stack([corner, beside]), jnp.stack([beside, corner]))
        total = jnp.broadcast_to(jnp.sum(corner * corner), (8, 128))
        for p in (1, 2, 4):
            total = total + send(total, across[p], f"total{p}")
        entries = n_row * count * kept * kept
        return enlarged, corner * lax.rsqrt(total[0, 0] / entries + 1e-06)

    placed = (P("row", "col", None), P("row", "col", None), P("row", None, None), P("row"))
    return jax.shard_map(
        body,
        mesh=mesh,
        in_specs=placed,
        out_specs=(P("row", "col", None), P("row", None, None)),
        check_vma=False,
    )
```

```python
import jax
import jax.numpy as jnp
from jax import lax
from jax.experimental import pallas as pl
from jax.experimental.pallas import tpu as pltpu
from jax.sharding import PartitionSpec as P

SIDE = 4


def start_gather(refs, where, off, scratch, sems, rows, at, sides):
    copies = []
    for k, (first, last) in enumerate(sides):
        column = []
        for n, (i, p) in enumerate(where):
            into = scratch.at[pl.ds(pl.multiple_of(off[n], 64), rows), first:last]
            source = refs[i].at[p, :, at[i] + first:at[i] + last]
            column.append(pltpu.make_async_copy(source, into, sems.at[k, n]))
        copies.append(column)
    for column in copies:
        for copy in column:
            copy.start()
    return copies


def product(offsets, lefts, pieces, at, width):
    rows, depth = lefts[0].shape
    sides = ((0, width),)
    where = [(i, p) for i, piece in enumerate(pieces) for p in range(piece.shape[0])]
    n_left = len(lefts)

    def kernel(off, *rest):
        ls, refs, outs = rest[:n_left], rest[n_left:n_left + len(pieces)], rest[n_left + len(pieces):-4]
        lhs, scratch, left_sems, sems = rest[-4:]
        loads = [pltpu.make_async_copy(ls[p], lhs.at[pl.ds(p * rows, rows)], left_sems.at[p]) for p in range(n_left)]
        for copy in loads:
            copy.start()
        copies = start_gather(refs, where, off, scratch, sems, rows, at, sides)
        for copy in loads:
            copy.wait()
        for column, (first, last) in zip(copies, sides):
            for copy in column:
                copy.wait()
            got = jnp.dot(lhs[...], scratch[:, first:last], preferred_element_type=jnp.float32)
            for p in range(n_left):
                outs[p][:, first:last] = got[p * rows:(p + 1) * rows]

    outside = pl.BlockSpec(memory_space=pltpu.HBM)
    inside = pl.BlockSpec(memory_space=pltpu.VMEM)
    return pl.pallas_call(
        kernel,
        in_specs=[pl.BlockSpec(memory_space=pltpu.SMEM)] + [outside] * (n_left + len(pieces)),
        out_specs=[inside] * n_left,
        out_shape=[jax.ShapeDtypeStruct((rows, width), jnp.float32)] * n_left,
        scratch_shapes=[
            pltpu.VMEM((n_left * rows, depth), jnp.bfloat16),
            pltpu.VMEM((depth, width), jnp.bfloat16),
            pltpu.SemaphoreType.DMA((n_left,)),
            pltpu.SemaphoreType.DMA((1, len(where))),
        ],
        cost_estimate=pl.CostEstimate(
            flops=2 * n_left * rows * depth * width,
            bytes_accessed=2 * depth * (n_left * rows + width) + 4 * n_left * rows * width,
            transcendentals=0,
        ),
        compiler_params=pltpu.CompilerParams(vmem_limit_bytes=56 << 20),
    )(offsets, *lefts, *pieces)


def share(offsets, lefts, chosen, pieces, extra):
    rows, depth = lefts[0].shape
    kept = extra // 2
    n_left = len(lefts)
    where = [(i, p) for i, piece in enumerate(pieces) for p in range(piece.shape[0])]

    def kernel(off, pick, *rest):
        ls, refs = rest[:n_left], rest[n_left:n_left + len(pieces)]
        out, lhs, scratch, left_sems, sems = rest[-5:]
        loads = [pltpu.make_async_copy(ls[p], lhs.at[pl.ds(p * rows, rows)], left_sems.at[p]) for p in range(n_left)]
        for copy in loads:
            copy.start()
        copies = start_gather(refs, where, off, scratch, sems, rows, [0] * len(pieces), ((0, extra),))
        for copy in loads + copies[0]:
            copy.wait()
        got = jnp.dot(lhs[...], scratch[...], preferred_element_type=jnp.float32)
        inner = got[:, :kept] + got[:, kept:]
        terms = []
        for p in range(n_left):
            left_over, term = inner[p * rows:(p + 1) * rows], None
            for _ in range(3):
                digit = left_over.astype(jnp.bfloat16)
                left_over = left_over - digit.astype(jnp.float32)
                part = jnp.dot(pick[p], digit, preferred_element_type=jnp.float32)
                term = part if term is None else term + part
            terms.append(term)
        out[...] = (terms[0] + terms[1]) + (terms[2] + terms[3])

    outside = pl.BlockSpec(memory_space=pltpu.HBM)
    inside = pl.BlockSpec(memory_space=pltpu.VMEM)
    return pl.pallas_call(
        kernel,
        in_specs=[pl.BlockSpec(memory_space=pltpu.SMEM), inside] + [outside] * (n_left + len(pieces)),
        out_specs=inside,
        out_shape=jax.ShapeDtypeStruct((kept, kept), jnp.float32),
        scratch_shapes=[
            pltpu.VMEM((n_left * rows, depth), jnp.bfloat16),
            pltpu.VMEM((depth, extra), jnp.bfloat16),
            pltpu.SemaphoreType.DMA((n_left,)),
            pltpu.SemaphoreType.DMA((1, len(where))),
        ],
        cost_estimate=pl.CostEstimate(
            flops=2 * n_left * rows * depth * extra,
            bytes_accessed=2 * depth * (n_left * rows + extra),
            transcendentals=0,
        ),
        compiler_params=pltpu.CompilerParams(vmem_limit_bytes=56 << 20),
    )(offsets, chosen, *lefts, *pieces)


def place(spots, blocks, shape, into=None):
    rows, width = blocks[0].shape
    n = len(blocks)

    def kernel(at, *rest):
        out, sems = rest[-2:]
        copies = []
        for k in range(n):
            start = pl.multiple_of(at[n + k], 128)
            copies.append(pltpu.make_async_copy(rest[k], out.at[at[k], :, pl.ds(start, width)], sems.at[k]))
        for copy in copies:
            copy.start()
        for copy in copies:
            copy.wait()

    anywhere = pl.BlockSpec(memory_space=pl.ANY)
    inside = pl.BlockSpec(memory_space=pltpu.VMEM)
    given = list(blocks) + ([] if into is None else [into])
    return pl.pallas_call(
        kernel,
        in_specs=[pl.BlockSpec(memory_space=pltpu.SMEM)] + [inside] * n + [anywhere] * (len(given) - n),
        out_specs=anywhere,
        out_shape=jax.ShapeDtypeStruct(shape, jnp.float32),
        scratch_shapes=[pltpu.SemaphoreType.DMA((n,))],
        input_output_aliases={} if into is None else {n + 1: 0},
        compiler_params=pltpu.CompilerParams(vmem_limit_bytes=8 << 20),
    )(spots, *given)


def solution(mesh):
    n_row, n_col = mesh.shape["row"], mesh.shape["col"]

    def pairs(move):
        found = []
        for row in range(n_row):
            for col in range(n_col):
                cx, cy = col // SIDE, col % SIDE
                g, h = (cy, cx) if row % 2 else (cx, cy)
                to, g, h = move(row, g, h)
                cx, cy = (h, g) if row % 2 else (g, h)
                if to != row:
                    cx, cy = col // SIDE, col % SIDE
                found.append((row * n_col + col, to * n_col + cx * SIDE + cy))
        return found

    along_g = {p: pairs(lambda row, g, h, p=p: (row, g ^ p, h)) for p in (1, 2, 3)}
    along_h = {p: pairs(lambda row, g, h, p=p: (row, g, h ^ p)) for p in (1, 2)}
    up = pairs(lambda row, g, h: (row, g, (h + 1) % SIDE))
    down = pairs(lambda row, g, h: (row, g, (h - 1) % SIDE))
    across_h = pairs(lambda row, g, h: (row, g, (h + 2) % SIDE))
    diagonal = pairs(lambda row, g, h: (row, g ^ 2, h ^ 2))
    across = {p: pairs(lambda row, g, h, p=p: (row ^ p, g, h)) for p in (1, 2, 4)}

    def send(value, table, name):
        with jax.named_scope(name):
            return lax.ppermute(value, ("row", "col"), table)

    def after(value, *others):
        return lax.optimization_barrier((value, *others))[0]

    def body(left_edge, right_edge, projector, sector_size):
        count, rows, depth = left_edge.shape
        kept = projector.shape[2]
        half = depth // 2
        width = half // 2
        odd = lax.axis_index("row") % 2
        col = lax.axis_index("col")
        cx, cy = col // SIDE, col % SIDE
        g = jnp.where(odd == 1, cy, cx)
        h = jnp.where(odd == 1, cx, cy)
        owner = lambda gg, hh: jnp.where(odd == 1, hh * SIDE + gg, gg * SIDE + hh)

        states = jnp.arange(depth, dtype=jnp.int32)
        live = (states[None, :] < sector_size[:, None]).astype(jnp.bfloat16)
        masked = projector * live[:, :, None]

        sector = g // 2
        mine = lax.dynamic_index_in_dim(left_edge, sector, 0, keepdims=False)
        other = lax.dynamic_index_in_dim(left_edge, 1 - sector, 0, keepdims=False)

        right_edge = after(right_edge, mine, other)
        seen = jnp.einsum("skj,sjq->skq", right_edge, masked, preferred_element_type=jnp.float32)
        top = lax.reduce_precision(seen, exponent_bits=8, mantissa_bits=7)
        shadow = jnp.concatenate([top, seen - top], axis=2).astype(jnp.bfloat16)

        def part(p):
            to = g ^ p
            got = lax.dynamic_slice(right_edge, (to // 2, 0, (to % 2) * half), (1, rows, half))[0]
            return jnp.concatenate([lax.dynamic_index_in_dim(shadow, to // 2, 0, keepdims=False), got], axis=1)

        gs = [g ^ p for p in range(SIDE)]
        hs = [h, (h - 1) % SIDE, (h + 1) % SIDE, (h + 2) % SIDE]
        offsets = jnp.stack([owner(gg, hh) * rows for hh in hs for gg in gs]).astype(jnp.int32)

        left = [mine] + [send(mine if p == 1 else other, along_g[p], f"left{p}") for p in (1, 2, 3)]
        blocks = [part(0)] + [send(part(p), along_g[p], f"right{p}") for p in (1, 2, 3)]

        extra = 2 * kept

        def cut(c):
            first = extra + width if c else 0
            return jnp.stack([block[:, first:extra + (c + 1) * width] for block in blocks])

        def put(c, out, into):
            first = c * width
            spots = jnp.stack([gg // 2 for gg in gs] + [(gg % 2) * half + first for gg in gs]).astype(jnp.int32)
            return place(spots, out, (count, rows, depth), into)

        def back(c, out):
            sent = {p: send(out[p], along_g[p], f"back{c}{p}") for p in (2, 1, 3)}
            return [out[0], sent[1], sent[2], sent[3]]

        ours = lax.dynamic_index_in_dim(masked, sector, 0, keepdims=False)
        chosen = jnp.stack([lax.dynamic_slice_in_dim(ours, owner(gg, h) * rows, rows, 0).T for gg in gs])

        shade = jnp.stack([block[:, :extra] for block in blocks])
        own0 = after(cut(0), left[1], left[3])
        far = send(shade, across_h, "shade")
        below0, above0 = send(own0, up, "up0"), send(own0, down, "down0")
        below0, above0, far, left[2] = lax.optimization_barrier((below0, above0, far, left[2]))
        own1 = cut(1)
        beyond0 = send(below0, up, "forward0")
        above1 = send(after(own1, above0), down, "down1")
        corner = share(offsets, left, chosen, (own0, below0, above0, far), extra)
        corner = corner + send(corner, along_h[1], "corner1")
        beyond0, above1, corner = lax.optimization_barrier((beyond0, above1, corner))
        below1 = send(after(own1, beyond0), up, "up1")
        beyond1 = send(above1, down, "forward1")
        around = [corner] + [send(corner, table, "around") for table in (along_h[2], along_g[2], diagonal)]
        skips = (extra,) * 4
        out0 = product(offsets, left, (own0, below0, above0, beyond0), skips, width)
        out0, around = lax.optimization_barrier((out0, around))
        out0 = back(0, out0)
        corner, beside = around[0] + around[1], around[2] + around[3]
        corner = jnp.where(sector == 0, jnp.stack([corner, beside]), jnp.stack([beside, corner]))
        total = after(jnp.broadcast_to(jnp.sum(corner * corner), (8, 128)), below1, beyond1)
        total = total + send(total, across[1], "total1")
        out1 = product(offsets, left, (own1, below1, above1, beyond1), (0,) * 4, width)
        first, total = lax.optimization_barrier((out1[0], total))
        out1 = [first] + [after(out1[p], out0[p], total) for p in (1, 2, 3)]
        out1 = back(1, out1)
        enlarged = put(1, out1, put(0, out0, None))
        for p in (2, 4):
            total = total + send(total, across[p], f"total{p}")
        entries = n_row * count * kept * kept
        return enlarged, corner * lax.rsqrt(total[0, 0] / entries + 1e-06)

    placed = (P("row", "col", None), P("row", "col", None), P("row", None, None), P("row"))
    return jax.shard_map(
        body,
        mesh=mesh,
        in_specs=placed,
        out_specs=(P("row", "col", None), P("row", None, None)),
        check_vma=False,
    )
```

```python
import jax
import jax.numpy as jnp
from jax import lax
from jax.experimental import pallas as pl
from jax.experimental.pallas import tpu as pltpu
from jax.sharding import PartitionSpec as P

SIDE = 4


def start_gather(refs, where, off, scratch, sems, rows, at, sides):
    copies = []
    for k, (first, last) in enumerate(sides):
        column = []
        for n, (i, p) in enumerate(where):
            into = scratch.at[pl.ds(pl.multiple_of(off[n], 64), rows), first:last]
            source = refs[i].at[p, :, at[i] + first:at[i] + last]
            column.append(pltpu.make_async_copy(source, into, sems.at[k, n]))
        copies.append(column)
    for column in copies:
        for copy in column:
            copy.start()
    return copies


def product(offsets, lefts, pieces, at, width):
    rows, depth = lefts[0].shape
    sides = ((0, width),)
    where = [(i, p) for i, piece in enumerate(pieces) for p in range(piece.shape[0])]
    n_left = len(lefts)

    def kernel(off, *rest):
        ls, refs, outs = rest[:n_left], rest[n_left:n_left + len(pieces)], rest[n_left + len(pieces):-4]
        lhs, scratch, left_sems, sems = rest[-4:]
        loads = [pltpu.make_async_copy(ls[p], lhs.at[pl.ds(p * rows, rows)], left_sems.at[p]) for p in range(n_left)]
        for copy in loads:
            copy.start()
        copies = start_gather(refs, where, off, scratch, sems, rows, at, sides)
        for copy in loads:
            copy.wait()
        for column, (first, last) in zip(copies, sides):
            for copy in column:
                copy.wait()
            got = jnp.dot(lhs[...], scratch[:, first:last], preferred_element_type=jnp.float32)
            for p in range(n_left):
                outs[p][:, first:last] = got[p * rows:(p + 1) * rows]

    outside = pl.BlockSpec(memory_space=pltpu.HBM)
    inside = pl.BlockSpec(memory_space=pltpu.VMEM)
    return pl.pallas_call(
        kernel,
        in_specs=[pl.BlockSpec(memory_space=pltpu.SMEM)] + [outside] * (n_left + len(pieces)),
        out_specs=[inside] * n_left,
        out_shape=[jax.ShapeDtypeStruct((rows, width), jnp.float32)] * n_left,
        scratch_shapes=[
            pltpu.VMEM((n_left * rows, depth), jnp.bfloat16),
            pltpu.VMEM((depth, width), jnp.bfloat16),
            pltpu.SemaphoreType.DMA((n_left,)),
            pltpu.SemaphoreType.DMA((1, len(where))),
        ],
        cost_estimate=pl.CostEstimate(
            flops=2 * n_left * rows * depth * width,
            bytes_accessed=2 * depth * (n_left * rows + width) + 4 * n_left * rows * width,
            transcendentals=0,
        ),
        compiler_params=pltpu.CompilerParams(vmem_limit_bytes=56 << 20),
    )(offsets, *lefts, *pieces)


def share(offsets, lefts, chosen, pieces, extra):
    rows, depth = lefts[0].shape
    kept = extra // 2
    n_left = len(lefts)
    where = [(i, p) for i, piece in enumerate(pieces) for p in range(piece.shape[0])]

    def kernel(off, pick, *rest):
        ls, refs = rest[:n_left], rest[n_left:n_left + len(pieces)]
        out, lhs, scratch, left_sems, sems = rest[-5:]
        loads = [pltpu.make_async_copy(ls[p], lhs.at[pl.ds(p * rows, rows)], left_sems.at[p]) for p in range(n_left)]
        for copy in loads:
            copy.start()
        copies = start_gather(refs, where, off, scratch, sems, rows, [0] * len(pieces), ((0, extra),))
        for copy in loads + copies[0]:
            copy.wait()
        got = jnp.dot(lhs[...], scratch[...], preferred_element_type=jnp.float32)
        inner = got[:, :kept] + got[:, kept:]
        terms = []
        for p in range(n_left):
            left_over, term = inner[p * rows:(p + 1) * rows], None
            for _ in range(3):
                digit = left_over.astype(jnp.bfloat16)
                left_over = left_over - digit.astype(jnp.float32)
                part = jnp.dot(pick[p], digit, preferred_element_type=jnp.float32)
                term = part if term is None else term + part
            terms.append(term)
        out[...] = (terms[0] + terms[1]) + (terms[2] + terms[3])

    outside = pl.BlockSpec(memory_space=pltpu.HBM)
    inside = pl.BlockSpec(memory_space=pltpu.VMEM)
    return pl.pallas_call(
        kernel,
        in_specs=[pl.BlockSpec(memory_space=pltpu.SMEM), inside] + [outside] * (n_left + len(pieces)),
        out_specs=inside,
        out_shape=jax.ShapeDtypeStruct((kept, kept), jnp.float32),
        scratch_shapes=[
            pltpu.VMEM((n_left * rows, depth), jnp.bfloat16),
            pltpu.VMEM((depth, extra), jnp.bfloat16),
            pltpu.SemaphoreType.DMA((n_left,)),
            pltpu.SemaphoreType.DMA((1, len(where))),
        ],
        cost_estimate=pl.CostEstimate(
            flops=2 * n_left * rows * depth * extra,
            bytes_accessed=2 * depth * (n_left * rows + extra),
            transcendentals=0,
        ),
        compiler_params=pltpu.CompilerParams(vmem_limit_bytes=56 << 20),
    )(offsets, chosen, *lefts, *pieces)


def place(spots, blocks, shape, into=None):
    rows, width = blocks[0].shape
    n = len(blocks)

    def kernel(at, *rest):
        out, sems = rest[-2:]
        copies = []
        for k in range(n):
            start = pl.multiple_of(at[n + k], 128)
            copies.append(pltpu.make_async_copy(rest[k], out.at[at[k], :, pl.ds(start, width)], sems.at[k]))
        for copy in copies:
            copy.start()
        for copy in copies:
            copy.wait()

    anywhere = pl.BlockSpec(memory_space=pl.ANY)
    inside = pl.BlockSpec(memory_space=pltpu.VMEM)
    given = list(blocks) + ([] if into is None else [into])
    return pl.pallas_call(
        kernel,
        in_specs=[pl.BlockSpec(memory_space=pltpu.SMEM)] + [inside] * n + [anywhere] * (len(given) - n),
        out_specs=anywhere,
        out_shape=jax.ShapeDtypeStruct(shape, jnp.float32),
        scratch_shapes=[pltpu.SemaphoreType.DMA((n,))],
        input_output_aliases={} if into is None else {n + 1: 0},
        compiler_params=pltpu.CompilerParams(vmem_limit_bytes=8 << 20),
    )(spots, *given)


def solution(mesh):
    n_row, n_col = mesh.shape["row"], mesh.shape["col"]

    def pairs(move):
        found = []
        for row in range(n_row):
            for col in range(n_col):
                cx, cy = col // SIDE, col % SIDE
                g, h = (cy, cx) if row % 2 else (cx, cy)
                to, g, h = move(row, g, h)
                cx, cy = (h, g) if row % 2 else (g, h)
                if to != row:
                    cx, cy = col // SIDE, col % SIDE
                found.append((row * n_col + col, to * n_col + cx * SIDE + cy))
        return found

    along_g = {p: pairs(lambda row, g, h, p=p: (row, g ^ p, h)) for p in (1, 2, 3)}
    along_h = {p: pairs(lambda row, g, h, p=p: (row, g, h ^ p)) for p in (1, 2)}
    up = pairs(lambda row, g, h: (row, g, (h + 1) % SIDE))
    down = pairs(lambda row, g, h: (row, g, (h - 1) % SIDE))
    across_h = pairs(lambda row, g, h: (row, g, (h + 2) % SIDE))
    diagonal = pairs(lambda row, g, h: (row, g ^ 2, h ^ 2))
    across = {p: pairs(lambda row, g, h, p=p: (row ^ p, g, h)) for p in (1, 2, 4)}

    def send(value, table, name):
        with jax.named_scope(name):
            return lax.ppermute(value, ("row", "col"), table)

    def after(value, *others):
        return lax.optimization_barrier((value, *others))[0]

    def body(left_edge, right_edge, projector, sector_size):
        count, rows, depth = left_edge.shape
        kept = projector.shape[2]
        half = depth // 2
        width = half // 2
        odd = lax.axis_index("row") % 2
        col = lax.axis_index("col")
        cx, cy = col // SIDE, col % SIDE
        g = jnp.where(odd == 1, cy, cx)
        h = jnp.where(odd == 1, cx, cy)
        owner = lambda gg, hh: jnp.where(odd == 1, hh * SIDE + gg, gg * SIDE + hh)

        states = jnp.arange(depth, dtype=jnp.int32)
        live = (states[None, :] < sector_size[:, None]).astype(jnp.bfloat16)
        masked = projector * live[:, :, None]

        sector = g // 2
        mine = lax.dynamic_index_in_dim(left_edge, sector, 0, keepdims=False)
        other = lax.dynamic_index_in_dim(left_edge, 1 - sector, 0, keepdims=False)

        right_edge = after(right_edge, mine, other)
        seen = jnp.einsum("skj,sjq->skq", right_edge, masked, preferred_element_type=jnp.float32)
        top = lax.reduce_precision(seen, exponent_bits=8, mantissa_bits=7)
        shadow = jnp.concatenate([top, seen - top], axis=2).astype(jnp.bfloat16)

        def part(p):
            to = g ^ p
            got = lax.dynamic_slice(right_edge, (to // 2, 0, (to % 2) * half), (1, rows, half))[0]
            return jnp.concatenate([lax.dynamic_index_in_dim(shadow, to // 2, 0, keepdims=False), got], axis=1)

        gs = [g ^ p for p in range(SIDE)]
        hs = [h, (h - 1) % SIDE, (h + 1) % SIDE, (h + 2) % SIDE]
        offsets = jnp.stack([owner(gg, hh) * rows for hh in hs for gg in gs]).astype(jnp.int32)

        left = [mine] + [send(mine if p == 1 else other, along_g[p], f"left{p}") for p in (1, 2, 3)]
        blocks = [part(0)] + [send(part(p), along_g[p], f"right{p}") for p in (1, 2, 3)]

        extra = 2 * kept

        def cut(c):
            first = extra + width if c else 0
            return jnp.stack([block[:, first:extra + (c + 1) * width] for block in blocks])

        def put(c, out, into):
            first = c * width
            spots = jnp.stack([gg // 2 for gg in gs] + [(gg % 2) * half + first for gg in gs]).astype(jnp.int32)
            return place(spots, out, (count, rows, depth), into)

        def back(c, out):
            sent = {p: send(out[p], along_g[p], f"back{c}{p}") for p in (2, 1, 3)}
            return [out[0], sent[1], sent[2], sent[3]]

        ours = lax.dynamic_index_in_dim(masked, sector, 0, keepdims=False)
        chosen = jnp.stack([lax.dynamic_slice_in_dim(ours, owner(gg, h) * rows, rows, 0).T for gg in gs])

        shade = jnp.stack([block[:, :extra] for block in blocks])
        own0 = after(cut(0), left[1], left[3])
        far = send(shade, across_h, "shade")
        below0, above0 = send(own0, up, "up0"), send(own0, down, "down0")
        below0, above0, far, left[2] = lax.optimization_barrier((below0, above0, far, left[2]))
        own1 = cut(1)
        beyond0 = send(below0, up, "forward0")
        above1 = send(after(own1, above0), down, "down1")
        corner = share(offsets, left, chosen, (own0, below0, above0, far), extra)
        corner = corner + send(corner, along_h[1], "corner1")
        beyond0, above1, corner = lax.optimization_barrier((beyond0, above1, corner))
        below1 = send(after(own1, beyond0), up, "up1")
        beyond1 = send(above1, down, "forward1")
        around = [corner] + [send(corner, table, "around") for table in (along_h[2], along_g[2], diagonal)]
        skips = (extra,) * 4
        out0 = product(offsets, left, (own0, below0, above0, beyond0), skips, width)
        longest = out0[2]
        out0, around = lax.optimization_barrier(([out0[0], out0[1], out0[3]], around))
        out0 = back(0, [out0[0], out0[1], longest, out0[2]])
        corner, beside = around[0] + around[1], around[2] + around[3]
        corner = jnp.where(sector == 0, jnp.stack([corner, beside]), jnp.stack([beside, corner]))
        total = after(jnp.broadcast_to(jnp.sum(corner * corner), (8, 128)), below1, beyond1)
        total = total + send(total, across[1], "total1")
        out1 = product(offsets, left, (own1, below1, above1, beyond1), (0,) * 4, width)
        first, total = lax.optimization_barrier((out1[0], total))
        out1 = [first, after(out1[1], *out0[1:]), after(out1[2], out0[2], total), after(out1[3], *out0[1:])]
        out1 = back(1, out1)
        enlarged = put(1, out1, put(0, out0, None))
        for p in (2, 4):
            total = total + send(total, across[p], f"total{p}")
        entries = n_row * count * kept * kept
        return enlarged, corner * lax.rsqrt(total[0, 0] / entries + 1e-06)

    placed = (P("row", "col", None), P("row", "col", None), P("row", None, None), P("row"))
    return jax.shard_map(
        body,
        mesh=mesh,
        in_specs=placed,
        out_specs=(P("row", "col", None), P("row", None, None)),
        check_vma=False,
    )
```

```python
import jax
import jax.numpy as jnp
from jax import lax
from jax.experimental import pallas as pl
from jax.experimental.pallas import tpu as pltpu
from jax.sharding import PartitionSpec as P

SIDE = 4


def start_gather(refs, where, off, scratch, sems, rows, at, sides):
    copies = []
    for k, (first, last) in enumerate(sides):
        column = []
        for n, (i, p) in enumerate(where):
            into = scratch.at[pl.ds(pl.multiple_of(off[n], 64), rows), first:last]
            source = refs[i].at[p, :, at[i] + first:at[i] + last]
            column.append(pltpu.make_async_copy(source, into, sems.at[k, n]))
        copies.append(column)
    for column in copies:
        for copy in column:
            copy.start()
    return copies


def product(offsets, lefts, pieces, at, width):
    rows, depth = lefts[0].shape
    sides = ((0, width),)
    where = [(i, p) for i, piece in enumerate(pieces) for p in range(piece.shape[0])]
    n_left = len(lefts)

    def kernel(off, *rest):
        ls, refs, outs = rest[:n_left], rest[n_left:n_left + len(pieces)], rest[n_left + len(pieces):-4]
        lhs, scratch, left_sems, sems = rest[-4:]
        loads = [pltpu.make_async_copy(ls[p], lhs.at[pl.ds(p * rows, rows)], left_sems.at[p]) for p in range(n_left)]
        for copy in loads:
            copy.start()
        copies = start_gather(refs, where, off, scratch, sems, rows, at, sides)
        for copy in loads:
            copy.wait()
        for column, (first, last) in zip(copies, sides):
            for copy in column:
                copy.wait()
            got = jnp.dot(lhs[...], scratch[:, first:last], preferred_element_type=jnp.float32)
            for p in range(n_left):
                outs[p][:, first:last] = got[p * rows:(p + 1) * rows]

    outside = pl.BlockSpec(memory_space=pltpu.HBM)
    inside = pl.BlockSpec(memory_space=pltpu.VMEM)
    return pl.pallas_call(
        kernel,
        in_specs=[pl.BlockSpec(memory_space=pltpu.SMEM)] + [outside] * (n_left + len(pieces)),
        out_specs=[inside] * n_left,
        out_shape=[jax.ShapeDtypeStruct((rows, width), jnp.float32)] * n_left,
        scratch_shapes=[
            pltpu.VMEM((n_left * rows, depth), jnp.bfloat16),
            pltpu.VMEM((depth, width), jnp.bfloat16),
            pltpu.SemaphoreType.DMA((n_left,)),
            pltpu.SemaphoreType.DMA((1, len(where))),
        ],
        cost_estimate=pl.CostEstimate(
            flops=2 * n_left * rows * depth * width,
            bytes_accessed=2 * depth * (n_left * rows + width) + 4 * n_left * rows * width,
            transcendentals=0,
        ),
        compiler_params=pltpu.CompilerParams(vmem_limit_bytes=56 << 20),
    )(offsets, *lefts, *pieces)


def share(offsets, lefts, chosen, pieces, extra):
    rows, depth = lefts[0].shape
    kept = extra // 2
    n_left = len(lefts)
    where = [(i, p) for i, piece in enumerate(pieces) for p in range(piece.shape[0])]

    def kernel(off, pick, *rest):
        ls, refs = rest[:n_left], rest[n_left:n_left + len(pieces)]
        out, lhs, scratch, left_sems, sems = rest[-5:]
        loads = [pltpu.make_async_copy(ls[p], lhs.at[pl.ds(p * rows, rows)], left_sems.at[p]) for p in range(n_left)]
        for copy in loads:
            copy.start()
        copies = start_gather(refs, where, off, scratch, sems, rows, [0] * len(pieces), ((0, extra),))
        for copy in loads + copies[0]:
            copy.wait()
        got = jnp.dot(lhs[...], scratch[...], preferred_element_type=jnp.float32)
        inner = got[:, :kept] + got[:, kept:]
        terms = []
        for p in range(n_left):
            left_over, term = inner[p * rows:(p + 1) * rows], None
            for _ in range(3):
                digit = left_over.astype(jnp.bfloat16)
                left_over = left_over - digit.astype(jnp.float32)
                part = jnp.dot(pick[p], digit, preferred_element_type=jnp.float32)
                term = part if term is None else term + part
            terms.append(term)
        out[...] = (terms[0] + terms[1]) + (terms[2] + terms[3])

    outside = pl.BlockSpec(memory_space=pltpu.HBM)
    inside = pl.BlockSpec(memory_space=pltpu.VMEM)
    return pl.pallas_call(
        kernel,
        in_specs=[pl.BlockSpec(memory_space=pltpu.SMEM), inside] + [outside] * (n_left + len(pieces)),
        out_specs=inside,
        out_shape=jax.ShapeDtypeStruct((kept, kept), jnp.float32),
        scratch_shapes=[
            pltpu.VMEM((n_left * rows, depth), jnp.bfloat16),
            pltpu.VMEM((depth, extra), jnp.bfloat16),
            pltpu.SemaphoreType.DMA((n_left,)),
            pltpu.SemaphoreType.DMA((1, len(where))),
        ],
        cost_estimate=pl.CostEstimate(
            flops=2 * n_left * rows * depth * extra,
            bytes_accessed=2 * depth * (n_left * rows + extra),
            transcendentals=0,
        ),
        compiler_params=pltpu.CompilerParams(vmem_limit_bytes=56 << 20),
    )(offsets, chosen, *lefts, *pieces)


def place(spots, blocks, shape, into=None):
    rows, width = blocks[0].shape
    n = len(blocks)

    def kernel(at, *rest):
        out, sems = rest[-2:]
        copies = []
        for k in range(n):
            start = pl.multiple_of(at[n + k], 128)
            copies.append(pltpu.make_async_copy(rest[k], out.at[at[k], :, pl.ds(start, width)], sems.at[k]))
        for copy in copies:
            copy.start()
        for copy in copies:
            copy.wait()

    anywhere = pl.BlockSpec(memory_space=pl.ANY)
    inside = pl.BlockSpec(memory_space=pltpu.VMEM)
    given = list(blocks) + ([] if into is None else [into])
    return pl.pallas_call(
        kernel,
        in_specs=[pl.BlockSpec(memory_space=pltpu.SMEM)] + [inside] * n + [anywhere] * (len(given) - n),
        out_specs=anywhere,
        out_shape=jax.ShapeDtypeStruct(shape, jnp.float32),
        scratch_shapes=[pltpu.SemaphoreType.DMA((n,))],
        input_output_aliases={} if into is None else {n + 1: 0},
        compiler_params=pltpu.CompilerParams(vmem_limit_bytes=8 << 20),
    )(spots, *given)


def solution(mesh):
    n_row, n_col = mesh.shape["row"], mesh.shape["col"]

    def pairs(move):
        found = []
        for row in range(n_row):
            for col in range(n_col):
                cx, cy = col // SIDE, col % SIDE
                g, h = (cy, cx) if row % 2 else (cx, cy)
                to, g, h = move(row, g, h)
                cx, cy = (h, g) if row % 2 else (g, h)
                if to != row:
                    cx, cy = col // SIDE, col % SIDE
                found.append((row * n_col + col, to * n_col + cx * SIDE + cy))
        return found

    along_g = {p: pairs(lambda row, g, h, p=p: (row, g ^ p, h)) for p in (1, 2, 3)}
    along_h = {p: pairs(lambda row, g, h, p=p: (row, g, h ^ p)) for p in (1, 2)}
    up = pairs(lambda row, g, h: (row, g, (h + 1) % SIDE))
    down = pairs(lambda row, g, h: (row, g, (h - 1) % SIDE))
    across_h = pairs(lambda row, g, h: (row, g, (h + 2) % SIDE))
    diagonal = pairs(lambda row, g, h: (row, g ^ 2, h ^ 2))
    across = {p: pairs(lambda row, g, h, p=p: (row ^ p, g, h)) for p in (1, 2, 4)}

    def send(value, table, name):
        with jax.named_scope(name):
            return lax.ppermute(value, ("row", "col"), table)

    def after(value, *others):
        return lax.optimization_barrier((value, *others))[0]

    def body(left_edge, right_edge, projector, sector_size):
        count, rows, depth = left_edge.shape
        kept = projector.shape[2]
        half = depth // 2
        width = half // 2
        odd = lax.axis_index("row") % 2
        col = lax.axis_index("col")
        cx, cy = col // SIDE, col % SIDE
        g = jnp.where(odd == 1, cy, cx)
        h = jnp.where(odd == 1, cx, cy)
        owner = lambda gg, hh: jnp.where(odd == 1, hh * SIDE + gg, gg * SIDE + hh)

        states = jnp.arange(depth, dtype=jnp.int32)
        live = (states[None, :] < sector_size[:, None]).astype(jnp.bfloat16)
        masked = projector * live[:, :, None]

        sector = g // 2
        mine = lax.dynamic_index_in_dim(left_edge, sector, 0, keepdims=False)
        other = lax.dynamic_index_in_dim(left_edge, 1 - sector, 0, keepdims=False)

        right_edge = after(right_edge, mine, other)
        seen = jnp.einsum("skj,sjq->skq", right_edge, masked, preferred_element_type=jnp.float32)
        top = lax.reduce_precision(seen, exponent_bits=8, mantissa_bits=7)
        shadow = jnp.concatenate([top, seen - top], axis=2).astype(jnp.bfloat16)

        def part(p):
            to = g ^ p
            got = lax.dynamic_slice(right_edge, (to // 2, 0, (to % 2) * half), (1, rows, half))[0]
            return jnp.concatenate([lax.dynamic_index_in_dim(shadow, to // 2, 0, keepdims=False), got], axis=1)

        gs = [g ^ p for p in range(SIDE)]
        hs = [h, (h - 1) % SIDE, (h + 1) % SIDE, (h + 2) % SIDE]
        offsets = jnp.stack([owner(gg, hh) * rows for hh in hs for gg in gs]).astype(jnp.int32)

        left = [mine] + [send(mine if p == 1 else other, along_g[p], f"left{p}") for p in (1, 2, 3)]
        blocks = [part(0)] + [send(part(p), along_g[p], f"right{p}") for p in (1, 2, 3)]

        extra = 2 * kept

        def cut(c):
            first = extra + width if c else 0
            return jnp.stack([block[:, first:extra + (c + 1) * width] for block in blocks])

        def put(c, out, into):
            first = c * width
            spots = jnp.stack([gg // 2 for gg in gs] + [(gg % 2) * half + first for gg in gs]).astype(jnp.int32)
            return place(spots, out, (count, rows, depth), into)

        def back(c, out):
            sent = {p: send(out[p], along_g[p], f"back{c}{p}") for p in (2, 1, 3)}
            return [out[0], sent[1], sent[2], sent[3]]

        ours = lax.dynamic_index_in_dim(masked, sector, 0, keepdims=False)
        chosen = jnp.stack([lax.dynamic_slice_in_dim(ours, owner(gg, h) * rows, rows, 0).T for gg in gs])

        shade = jnp.stack([block[:, :extra] for block in blocks])
        own0 = after(cut(0), left[1], left[3])
        far = send(shade, across_h, "shade")
        below0, above0 = send(own0, up, "up0"), send(own0, down, "down0")
        below0, above0, far, left[2] = lax.optimization_barrier((below0, above0, far, left[2]))
        own1 = cut(1)
        beyond0 = send(below0, up, "forward0")
        above1 = send(after(own1, above0), down, "down1")
        corner = share(offsets, left, chosen, (own0, below0, above0, far), extra)
        corner = corner + send(corner, along_h[1], "corner1")
        beyond0, above1, corner = lax.optimization_barrier((beyond0, above1, corner))
        below1 = send(after(own1, beyond0), up, "up1")
        beyond1 = send(above1, down, "forward1")
        around = [corner] + [send(corner, table, "around") for table in (along_h[2], along_g[2], diagonal)]
        skips = (extra,) * 4
        out0 = product(offsets, left, (own0, below0, above0, beyond0), skips, width)
        longest = out0[2]
        out0, around = lax.optimization_barrier(([out0[0], out0[1], out0[3]], around))
        out0 = back(0, [out0[0], out0[1], longest, out0[2]])
        corner, beside = around[0] + around[1], around[2] + around[3]
        corner = jnp.where(sector == 0, jnp.stack([corner, beside]), jnp.stack([beside, corner]))
        total = after(jnp.broadcast_to(jnp.sum(corner * corner), (8, 128)), below1, beyond1)
        total = total + send(total, across[1], "total1")
        out1 = product(offsets, left, (own1, below1, above1, beyond1), (0,) * 4, width)
        first, total = lax.optimization_barrier((out1[0], total))
        out1 = [first, after(out1[1], *out0[1:]), after(out1[2], out0[2]), after(out1[3], *out0[1:])]
        out1 = back(1, out1)
        enlarged = put(1, out1, put(0, out0, None))
        for p in (2, 4):
            total = total + send(total, across[p], f"total{p}")
        entries = n_row * count * kept * kept
        return enlarged, corner * lax.rsqrt(total[0, 0] / entries + 1e-06)

    placed = (P("row", "col", None), P("row", "col", None), P("row", None, None), P("row"))
    return jax.shard_map(
        body,
        mesh=mesh,
        in_specs=placed,
        out_specs=(P("row", "col", None), P("row", None, None)),
        check_vma=False,
    )
```
